32 devices in a mesh: ia: 8 (over z, x), ja: 4 (over y, core).
Axes of the slice: x: 2, y: 2, z: 4, core: 2. Of those that a mesh axis runs over, the one named last changes fastest.
Arguments:
- amplitudes: bfloat16 [4, 8, 32, 128, 128], P(None, 'ia', 'ja'), may hold values from -6 to 6
- coefficients: bfloat16 [4, 8, 32, 128, 128], P(None, 'ia', 'ja'), may hold values from -0.5 to 0.5
- integrals: bfloat16 [4, 8, 32, 128, 128], P(None, 'ia', 'ja'), may hold values from -6 to 6
- pno_energy: float32 [4, 8, 32, 128], P(None, 'ia', 'ja'), may hold values from 0.5 to 4
- pno_counts: int32 [4, 8, 32], P(None, 'ia', 'ja'), may hold values from 32 to 128
- coupled: int32 [4, 8, 32, 12], P(None, 'ia', 'ja'), may hold values 0 or 1
- occ_fock: float32 [32, 32], replicated, may hold values from -1.5 to 1.5
- occ_energy: float32 [32], replicated, may hold values from -1.5 to -0.3
Outputs:
- amplitudes_next: bfloat16 [4, 8, 32, 128, 128], P(None, 'ia', 'ja')
The draws below stay inside these ranges and needn't reach their ends.
All inputs are finite; a program needn't handle non-finite values. No bound on the sum of `coupled` on one device may be relied on, other than what follows from the above.
Results may differ from the reference program's by a relative error of at most 0.0051.
Values may be sent and summed in bfloat16 or wider, within the bound.
A program may use at most 128 MiB of HBM per device.

```python
from functools import partial
import jax
import jax.numpy as jnp
from jax import lax

V = 128
WIN = 6
ITERS = 2
BLOCK = 8
BLOCKS = 4
NOCC = 32


def set_ends(drawn, rng, low, top_value):
    dims = drawn.shape
    place = [jax.random.randint(jax.random.fold_in(rng, axis), (), 0, dims[axis]) for axis in range(len(dims))]
    drawn = drawn.at[tuple(place)].set(low)
    longest = dims.index(max(dims))
    place[longest] = (place[longest] + 1) % dims[longest]
    return drawn.at[tuple(place)].set(top_value)


def block_scale(rng, extent, pieces, low, largest):
    level = 1.0
    for dim, blocks in pieces:
        draws = jax.random.uniform(jax.random.fold_in(jax.random.fold_in(rng, 6), dim), (blocks,), jnp.float32, low / len(pieces), largest / len(pieces))
        level = level * jnp.repeat(jnp.exp(draws), extent[dim] // blocks).reshape((-1,) + (1,) * (len(extent) - 1 - dim))
    return level


def gaussian(own_key, shape, deviation, reach, shards=(), held_as=jnp.bfloat16):
    values = jax.random.normal(own_key, shape, jnp.float32) * deviation
    if len(shards) > 0:
        values = block_scale(own_key, shape, shards, -0.22, 0.18) * values
    return jnp.clip(values, min=-reach, max=reach).astype(held_as)


def setup_inputs(seed: int = 0) -> dict:
    seeds = jax.random.split(jax.random.key(seed), 9)
    amplitudes = gaussian(seeds[0], (BLOCKS, BLOCK, NOCC, V, V), 1.0, 6.0, ((1, 8), (2, 4)))
    coefficients = gaussian(seeds[1], (BLOCKS, BLOCK, NOCC, V, V), V ** -0.5, 0.5, ((1, 8), (2, 4)))
    integrals = gaussian(seeds[2], (BLOCKS, BLOCK, NOCC, V, V), 1.0, 6.0, ((1, 8), (2, 4)))
    pno_energy = jnp.clip(0.5 + 3.5 * jax.random.uniform(seeds[3], (BLOCKS, BLOCK, NOCC, V), jnp.float32) ** block_scale(seeds[3], (BLOCKS, BLOCK, NOCC, V), ((1, 8), (2, 4)), -0.2, 0.2), 0.5, 4.0)
    pno_counts = set_ends(jax.random.randint(seeds[4], (BLOCKS, BLOCK, NOCC), V // 4, V + 1), jax.random.fold_in(seeds[4], 1), V // 4, V).astype(jnp.int32)
    coupled = set_ends((jax.random.randint(seeds[5], (BLOCKS, BLOCK, NOCC, 2 * WIN), 0, 4) < 3).astype(jnp.int32), jax.random.fold_in(seeds[5], 1), 0, 1)
    occ_fock = gaussian(seeds[6], (NOCC, NOCC), 0.25, 1.5, (), jnp.float32)
    occ_energy = jnp.clip(jax.random.uniform(seeds[7], (NOCC,), jnp.float32, -1.5, -0.3), -1.5, -0.3)
    return dict(amplitudes=amplitudes, coefficients=coefficients, integrals=integrals, pno_energy=pno_energy, pno_counts=pno_counts, coupled=coupled, occ_fock=occ_fock, occ_energy=occ_energy)


DAMPING = 0.5


def window_shift(slot_index):
    return slot_index - WIN if slot_index < WIN else slot_index - WIN + 1


def rounded(values):
    return lax.optimization_barrier(values.astype(jnp.bfloat16)).astype(jnp.float32)


def fock_band(occ_fock):
    orbitals = occ_fock.shape[0]
    places = jnp.arange(orbitals, dtype=jnp.int32)
    rows_out = []
    for slot_index in range(2 * WIN):
        matches = places[:, None] == places[None, :] + window_shift(slot_index)
        rows_out.append(jnp.sum(jnp.where(matches, occ_fock, jnp.zeros_like(occ_fock)), axis=0))
    return jnp.stack(rows_out, axis=0)


def pair_mask(counts):
    levels = jnp.arange(V, dtype=jnp.int32)
    inside = levels[None, :] < counts[:, None]
    return inside[:, :, None] & inside[:, None, :]


def half_row(packed):
    amp_row, coef_row, integral_row, weights_row = packed
    amps_float = amp_row.astype(jnp.float32)
    coefs_float = coef_row.astype(jnp.float32)
    ints_float = integral_row.astype(jnp.float32)
    orbitals = amp_row.shape[0]
    leading = rounded(jnp.einsum("jab,jbc->jac", coefs_float, amps_float))
    back_form = jnp.einsum("jac,jdc->jad", leading, coefs_float).astype(jnp.bfloat16)
    padded = jnp.pad(back_form, ((WIN, WIN), (0, 0), (0, 0)))
    window_sum = jnp.zeros((orbitals, V, V), jnp.float32)
    for slot_index in range(2 * WIN):
        begin_at = WIN + window_shift(slot_index)
        window_sum = window_sum + weights_row[:, slot_index][:, None, None] * padded[begin_at:begin_at + orbitals].astype(jnp.float32)
    window_bf = rounded(window_sum)
    left_proj = rounded(jnp.einsum("jca,jcd->jad", coefs_float, window_bf))
    projected = jnp.einsum("jad,jde->jae", left_proj, coefs_float)
    left_quad = rounded(jnp.einsum("jab,jbc->jac", amps_float, ints_float))
    quadratic = jnp.einsum("jac,jcd->jad", left_quad, amps_float) / V
    return (0.5 * ints_float + quadratic - projected).astype(jnp.bfloat16)


def update_row(halves, occ_energy, packed):
    row_index, amp_row, energy_row, count_row = packed
    own_half = lax.dynamic_index_in_dim(halves, row_index, 0, keepdims=False)
    partner = lax.dynamic_index_in_dim(halves, row_index, 1, keepdims=False)
    residual = own_half.astype(jnp.float32) + jnp.swapaxes(partner, 1, 2).astype(jnp.float32)
    energy_own = lax.dynamic_index_in_dim(occ_energy, row_index, 0, keepdims=False)
    denominator = energy_row[:, :, None] + energy_row[:, None, :] - energy_own - occ_energy[:, None, None]
    stepped = (1.0 - DAMPING) * amp_row.astype(jnp.float32) - DAMPING * residual / denominator
    return jnp.where(pair_mask(count_row), stepped, jnp.zeros_like(stepped)).astype(jnp.bfloat16)


def mask_row(packed):
    amp_row, count_row = packed
    return jnp.where(pair_mask(count_row), amp_row, jnp.zeros_like(amp_row))


def reference(amplitudes, coefficients, integrals, pno_energy, pno_counts, coupled, occ_fock, occ_energy):
    orbitals = NOCC
    pair_shape = (orbitals, orbitals, V, V)
    amp_pairs = amplitudes.reshape(pair_shape)
    coef_pairs = coefficients.reshape(pair_shape)
    integral_pairs = integrals.reshape(pair_shape)
    energies = pno_energy.reshape(orbitals, orbitals, V)
    counts = pno_counts.reshape(orbitals, orbitals)
    listed = coupled.reshape(orbitals, orbitals, 2 * WIN).astype(jnp.float32)
    weights = listed * jnp.transpose(fock_band(occ_fock))[None, :, :]
    current = lax.map(mask_row, (amp_pairs, counts))
    row_ids = jnp.arange(orbitals, dtype=jnp.int32)
    for sweep in range(ITERS):
        halves = lax.map(half_row, (current, coef_pairs, integral_pairs, weights))
        current = lax.map(partial(update_row, halves, occ_energy), (row_ids, current, energies, counts))
    return current.reshape(amplitudes.shape)
```

```python
import functools

import jax
import jax.numpy as jnp
from jax import lax
from jax.experimental import pallas as pl
from jax.experimental.pallas import tpu as pltpu
from jax.sharding import PartitionSpec as P

WIN = 6
ITERS = 2
DAMPING = 0.5
GROUP = 4
MESH = pl.DeviceIdType.MESH
F32 = jnp.float32
BF16 = jnp.bfloat16


def window_shift(slot):
    return slot - WIN if slot < WIN else slot - WIN + 1


def dot(a, b):
    return jnp.dot(a, b, preferred_element_type=F32)


def sweeps_kernel(
    n_ia, n_ja,
    t_hbm, c_hbm, k_hbm, e_hbm, cnt_hbm, cpl_hbm, fock_hbm, occ_hbm,
    out_ref,
    c_ref, k_ref, e_ref, cnt_ref, cpl_ref, fock_ref, occ_ref,
    ct, xl, left, right, hq, gain, hs, hr,
    halo_send, halo_recv, pair_send, pair_recv, load_sem, small_sem, near_sem, go_sem,
):
    rows, cols, size, _ = out_ref.shape
    orbitals = occ_ref.shape[0]
    ia = lax.axis_index("ia")
    ja = lax.axis_index("ja")
    me = ia * n_ja + ja
    total = n_ia * n_ja
    mixed = [n // 2 + n % 2 * (cols // 2) for n in range(cols)]
    groups = [mixed[g : g + GROUP] for g in range(0, cols, GROUP)]
    core = ja % 2
    half_ja = n_ja // 2
    low = ja < half_ja
    border = (ja == half_ja - 1) | (ja == half_ja)

    def flipped(turn, f):
        return jnp.where(turn, n_ja - 1 - f, f)

    def first_at(step):
        return flipped(ja // 2 % 2 == 1, jnp.where(step % 2 == 0, step // 2, n_ja - 1 - step // 2))

    def send_at(step):
        return flipped(core == 1, step)

    def early_at(step):
        return 2 * step + jnp.where(low, 0, 1)

    def late_at(step):
        return 2 * step + jnp.where(low, 1, 0)

    def last_at(step):
        return (step + core * half_ja) % n_ja

    small = [
        pltpu.make_async_copy(src, dst, small_sem.at[n])
        for n, (src, dst) in enumerate(
            [(cnt_hbm, cnt_ref), (cpl_hbm, cpl_ref), (fock_hbm, fock_ref),
             (occ_hbm, occ_ref), (e_hbm, e_ref)]
        )
    ]

    def load(f, n):
        src, dst = [(t_hbm, out_ref), (c_hbm, c_ref), (k_hbm, k_ref)][n]
        return pltpu.make_async_copy(src.at[f], dst.at[f], load_sem.at[n, f])

    for copy in small:
        copy.start()
    for step in range(rows):
        f = first_at(step)
        load(f, 0).start()
        load(f, 1).start()
    for step in range(rows):
        load(send_at(step), 2).start()

    barrier = pltpu.get_barrier_semaphore()

    def greet_at(i, j):
        pl.semaphore_signal(barrier, inc=1, device_id=(i, j), device_id_type=MESH)

    def tell(sem, j):
        pl.semaphore_signal(sem, inc=1, device_id=(ia, j), device_id_type=MESH)

    @pl.when(core == 0)
    def _():
        greet_at(ia, ja + 1)

        @pl.when(ja > 0)
        def _():
            greet_at(ia, ja - 1)

    def greet_chips(step, carry):
        peer = (me // 2 + step) % (total // 2) * 2
        greet_at(peer // n_ja, peer % n_ja)
        return carry

    lax.fori_loop(1, total // 2, greet_chips, 0)

    @pl.when(ja == 0)
    def _():
        left[...] = jnp.zeros_like(left)

    @pl.when(ja == n_ja - 1)
    def _():
        right[...] = jnp.zeros_like(right)

    def to_right(sweep, f):
        return pltpu.make_async_remote_copy(
            src_ref=xl.at[f, pl.ds(cols - WIN, WIN)],
            dst_ref=left.at[sweep, f],
            send_sem=halo_send.at[0, f],
            recv_sem=halo_recv.at[sweep, 0, f],
            device_id=(ia, jnp.minimum(ja + 1, n_ja - 1)),
            device_id_type=MESH,
        )

    def to_left(sweep, f):
        return pltpu.make_async_remote_copy(
            src_ref=xl.at[f, pl.ds(0, WIN)],
            dst_ref=right.at[sweep, f],
            send_sem=halo_send.at[1, f],
            recv_sem=halo_recv.at[sweep, 1, f],
            device_id=(ia, jnp.maximum(ja - 1, 0)),
            device_id_type=MESH,
        )

    def start_halo(sweep, f):
        @pl.when(ja < n_ja - 1)
        def _():
            to_right(sweep, f).start()

        @pl.when(ja > 0)
        def _():
            to_left(sweep, f).start()

    def wait_halo(sweep, f):
        @pl.when(ja > 0)
        def _():
            to_right(sweep, f).wait_recv()

        @pl.when(ja < n_ja - 1)
        def _():
            to_left(sweep, f).wait_recv()

    def wait_halo_sends(sweep, f):
        @pl.when(ja < n_ja - 1)
        def _():
            to_right(sweep, f).wait_send()

        @pl.when(ja > 0)
        def _():
            to_left(sweep, f).wait_send()

    def pair_copy(sweep, f, c):
        return pltpu.make_async_remote_copy(
            src_ref=hs.at[f, c],
            dst_ref=hr.at[sweep, ja, ia],
            send_sem=pair_send.at[f, c],
            recv_sem=pair_recv.at[sweep, ja],
            device_id=(c, f),
            device_id_type=MESH,
        )

    def start_pair(sweep, f, c):
        own = (f == ja) & (c == ia)

        @pl.when(jnp.logical_not(own))
        def _():
            pair_copy(sweep, f, c).start()

        @pl.when(own)
        def _():
            pltpu.make_async_copy(
                hs.at[f, c], hr.at[sweep, ja, ia], pair_recv.at[sweep, ja]
            ).start()

    def wait_pair_row(sweep, f):
        pltpu.make_async_copy(hr.at[sweep, f], hr.at[sweep, f], pair_recv.at[sweep, f]).wait()

    def wait_pair_sends(sweep, f):
        for c in range(cols):
            @pl.when(jnp.logical_not((f == ja) & (c == ia)))
            def _():
                pair_copy(sweep, f, c).wait_send()

    def back_form(f, group):
        lead = [dot(c_ref[f, c], out_ref[f, c]).astype(BF16) for c in group]
        for y, c in zip(lead, group):
            xl[f, c] = dot(y, ct[f, c]).astype(BF16)

    def inside(f, c):
        count = cnt_ref[f, c]
        p = lax.broadcasted_iota(jnp.int32, (size, size), 0)
        q = lax.broadcasted_iota(jnp.int32, (size, size), 1)
        return (p < count) & (q < count)

    def meet_neighbours():
        @pl.when(core == 1)
        def _():
            pl.semaphore_wait(barrier, jnp.where(ja + 1 < n_ja, 2, 1))
            tell(near_sem, ja - 1)

            @pl.when(ja + 1 < n_ja)
            def _():
                tell(near_sem, ja + 1)

        @pl.when(core == 0)
        def _():
            pl.semaphore_wait(near_sem, jnp.where(ja > 0, 2, 1))

    def meet_all():
        @pl.when(core == 0)
        def _():
            pl.semaphore_wait(barrier, total - 2)
            tell(go_sem, ja + 1)

        @pl.when(core == 1)
        def _():
            pl.semaphore_wait(go_sem, 1)

    def first_rows(step, carry):
        f = first_at(step)
        load(f, 0).wait()
        load(f, 1).wait()
        for group in groups:
            for c in group:
                t = out_ref[f, c]
                out_ref[f, c] = jnp.where(inside(f, c), t, jnp.zeros_like(t))
                ct[f, c] = c_ref[f, c].T
            back_form(f, group)

        @pl.when(step == 0)
        def _():
            meet_neighbours()

        start_halo(0, f)
        return carry

    for copy in small:
        copy.wait()
    lax.fori_loop(0, rows, first_rows, 0)

    def gain_row(step, carry):
        f = step
        columns_e = e_ref[f].T
        for c in range(cols):
            shift = occ_ref[f * n_ia + ia] + occ_ref[ja * cols + c]
            denominator = columns_e[:, c : c + 1] + e_ref[f, pl.ds(c, 1)] - shift
            gain[f, c] = jnp.where(inside(f, c), DAMPING / denominator, 0.0)
        return carry

    def quad_row(f):
        for group in groups:
            z = [dot(out_ref[f, c], k_ref[f, c]).astype(BF16) for c in group]
            for left_quad, c in zip(z, group):
                hq[f, c] = 0.5 * k_ref[f, c].astype(F32) + dot(left_quad, out_ref[f, c]) * (1.0 / size)

    def half_row(sweep, at, step, carry, send=True):
        f = at(step)
        wait_halo(sweep, f)
        if sweep > 0:
            wait_pair_sends(sweep - 1, f)
        def run(group):
            sums = []
            for c in group:
                acc = None
                j = ja * cols + c
                for slot in range(2 * WIN):
                    d = window_shift(slot)
                    k = j + d
                    ok = (k >= 0) & (k < orbitals)
                    kc = jnp.clip(k, 0, orbitals - 1)
                    w = cpl_ref[f, c, slot].astype(F32) * fock_ref[kc, j]
                    w = jnp.where(ok, w, 0.0)
                    at = c + d
                    if at < 0:
                        x = left[sweep, f, at + WIN]
                    elif at >= cols:
                        x = right[sweep, f, at - cols]
                    else:
                        x = xl[f, at]
                    term = w * x.astype(F32)
                    acc = term if acc is None else acc + term
                sums.append(acc.astype(BF16))
            proj = [dot(ct[f, c], a).astype(BF16) for a, c in zip(sums, group)]
            for b, c in zip(proj, group):
                hs[f, c] = (hq[f, c] - dot(b, c_ref[f, c])).astype(BF16)
            if send:
                for c in group:
                    start_pair(sweep, f, c)

        for group in groups:
            run(group)
        return carry

    def update_row(sweep, at, step, carry):
        f = at(step)
        wait_pair_row(sweep, f)
        if sweep < ITERS - 1:
            wait_halo_sends(sweep, f)
        for group in groups:
            for c in group:
                resid = hs[f, c].astype(F32) + hr[sweep, f, c].T.astype(F32)
                out_ref[f, c] = (
                    (1.0 - DAMPING) * out_ref[f, c].astype(F32) - gain[f, c] * resid
                ).astype(BF16)
            if sweep < ITERS - 1:
                back_form(f, group)
        if sweep < ITERS - 1:
            start_halo(sweep + 1, f)
        return carry

    def first_half(step, carry, send=True):
        f = send_at(step)
        load(f, 2).wait()
        quad_row(f)
        return half_row(0, send_at, step, carry, send)

    def send_row(sweep, f):
        for c in mixed:
            start_pair(sweep, f, c)

    def quad_at(at, step, carry):
        quad_row(at(step))
        return carry

    def each(body, *args):
        lax.fori_loop(0, half_ja, functools.partial(body, *args), 0)

    meet_all()
    lax.fori_loop(0, rows - 1, first_half, 0)
    first_half(rows - 1, 0, send=False)
    lax.fori_loop(0, rows, gain_row, 0)
    held = send_at(rows - 1)
    for sweep in range(ITERS - 1):
        each(update_row, sweep, early_at)
        send_row(sweep, held)
        each(quad_at, early_at)

        @pl.when(border)
        def _():
            each(update_row, sweep, late_at)

        half = functools.partial(half_row, sweep + 1, early_at)
        lax.fori_loop(0, half_ja - 1, half, 0)
        half(half_ja - 1, 0)

        @pl.when(jnp.logical_not(border))
        def _():
            each(update_row, sweep, late_at)

        each(quad_at, late_at)
        half = functools.partial(half_row, sweep + 1, late_at)
        if sweep < ITERS - 2:
            lax.fori_loop(0, half_ja - 1, half, 0)
            half(half_ja - 1, 0, send=False)
            held = late_at(half_ja - 1)
        else:
            lax.fori_loop(0, half_ja, half, 0)
    lax.fori_loop(0, rows, functools.partial(update_row, ITERS - 1, last_at), 0)

    def finish(f, carry):
        wait_halo_sends(ITERS - 1, f)
        wait_pair_sends(ITERS - 1, f)
        return carry

    lax.fori_loop(0, rows, finish, 0)


def solution(mesh):
    n_ia, n_ja = mesh.shape["ia"], mesh.shape["ja"]

    def on_device(amps, coefs, ints, energy, counts, coupled, occ_fock, occ_energy):
        rows, _, cols, size, _ = amps.shape
        assert rows == n_ja and cols == n_ia and cols >= WIN and n_ja % 2 == 0
        pairs = (rows, cols, size, size)
        unit = 2 * rows * cols * size * size
        halo = 2 * ITERS * unit * WIN // cols
        limit = min(67043328, (9 + ITERS) * unit + halo + (4 << 20))
        out = pl.pallas_call(
            functools.partial(sweeps_kernel, n_ia, n_ja),
            out_shape=pltpu.VMEM(pairs, BF16),
            in_specs=[pl.BlockSpec(memory_space=pltpu.HBM)] * 8,
            out_specs=pl.BlockSpec(memory_space=pltpu.VMEM),
            scratch_shapes=[
                pltpu.VMEM(pairs, BF16),
                pltpu.VMEM(pairs, BF16),
                pltpu.VMEM((rows, cols, size), F32),
                pltpu.SMEM((rows, cols), jnp.int32),
                pltpu.SMEM((rows, cols, 2 * WIN), jnp.int32),
                pltpu.SMEM(occ_fock.shape, F32),
                pltpu.SMEM(occ_energy.shape, F32),
                pltpu.VMEM(pairs, BF16),
                pltpu.VMEM(pairs, BF16),
                pltpu.VMEM((ITERS, rows, WIN, size, size), BF16),
                pltpu.VMEM((ITERS, rows, WIN, size, size), BF16),
                pltpu.VMEM(pairs, F32),
                pltpu.VMEM(pairs, F32),
                pltpu.VMEM(pairs, BF16),
                pltpu.VMEM((ITERS,) + pairs, BF16),
                pltpu.SemaphoreType.DMA((2, rows)),
                pltpu.SemaphoreType.DMA((ITERS, 2, rows)),
                pltpu.SemaphoreType.DMA((rows, cols)),
                pltpu.SemaphoreType.DMA((ITERS, rows)),
                pltpu.SemaphoreType.DMA((3, rows)),
                pltpu.SemaphoreType.DMA((5,)),
                pltpu.SemaphoreType.REGULAR,
                pltpu.SemaphoreType.REGULAR,
            ],
            compiler_params=pltpu.CompilerParams(
                collective_id=0, has_side_effects=True, vmem_limit_bytes=limit
            ),
        )(*[
            pltpu.with_memory_space_constraint(x, pltpu.HBM)
            for x in (
                amps.reshape(pairs),
                coefs.reshape(pairs),
                ints.reshape(pairs),
                energy.reshape(rows, cols, size),
                counts.reshape(rows, cols),
                coupled.reshape(rows, cols, 2 * WIN),
                occ_fock,
                occ_energy,
            )
        ])
        return out.reshape(amps.shape)

    placed = (
        P(None, "ia", "ja", None, None),
        P(None, "ia", "ja", None, None),
        P(None, "ia", "ja", None, None),
        P(None, "ia", "ja", None),
        P(None, "ia", "ja"),
        P(None, "ia", "ja", None),
        P(),
        P(),
    )
    return jax.shard_map(
        on_device,
        mesh=mesh,
        in_specs=placed,
        out_specs=P(None, "ia", "ja", None, None),
        check_vma=False,
    )
```

```python
import functools

import jax
import jax.numpy as jnp
from jax import lax
from jax.experimental import pallas as pl
from jax.experimental.pallas import tpu as pltpu
from jax.sharding import PartitionSpec as P

WIN = 6
ITERS = 2
DAMPING = 0.5
GROUP = 4
MESH = pl.DeviceIdType.MESH
F32 = jnp.float32
BF16 = jnp.bfloat16


def window_shift(slot):
    return slot - WIN if slot < WIN else slot - WIN + 1


def dot(a, b):
    return jnp.dot(a, b, preferred_element_type=F32)


def sweeps_kernel(
    n_ia, n_ja,
    t_hbm, c_hbm, k_hbm, e_hbm, cnt_hbm, cpl_hbm, fock_hbm, occ_hbm,
    out_ref,
    c_ref, k_ref, e_ref, cnt_ref, cpl_ref, fock_ref, occ_ref,
    ct, xl, left, right, hq, gain, hs, hr,
    halo_send, halo_recv, pair_send, pair_recv, load_sem, small_sem, near_sem, go_sem,
):
    rows, cols, size, _ = out_ref.shape
    orbitals = occ_ref.shape[0]
    ia = lax.axis_index("ia")
    ja = lax.axis_index("ja")
    me = ia * n_ja + ja
    total = n_ia * n_ja
    mixed = [n // 2 + n % 2 * (cols // 2) for n in range(cols)]
    groups = [mixed[g : g + GROUP] for g in range(0, cols, GROUP)]
    core = ja % 2
    half_ja = n_ja // 2
    low = ja < half_ja
    border = (ja == half_ja - 1) | (ja == half_ja)

    def flipped(turn, f):
        return jnp.where(turn, n_ja - 1 - f, f)

    def middle_out(step):
        return half_ja + jnp.where(step % 2 == 0, -1 - step // 2, step // 2)

    def first_at(step):
        return flipped(low == border, middle_out(step))

    def send_at(step):
        return flipped(jnp.logical_not(low), middle_out(step))

    def own_at(step):
        return flipped(jnp.logical_not(low), step)

    def across_at(step):
        return flipped(jnp.logical_not(low), half_ja + step)

    def across_end_at(step):
        return across_at(jnp.where(core >= 0, half_ja - 1 - step, step))

    def last_at(step):
        return flipped(jnp.logical_not(low), jnp.where(step < half_ja, step, n_ja - 1 - step + half_ja))

    small = [
        pltpu.make_async_copy(src, dst, small_sem.at[n])
        for n, (src, dst) in enumerate(
            [(cnt_hbm, cnt_ref), (cpl_hbm, cpl_ref), (fock_hbm, fock_ref),
             (occ_hbm, occ_ref), (e_hbm, e_ref)]
        )
    ]

    def load(f, n):
        src, dst = [(t_hbm, out_ref), (c_hbm, c_ref), (k_hbm, k_ref)][n]
        return pltpu.make_async_copy(src.at[f], dst.at[f], load_sem.at[n, f])

    for copy in small:
        copy.start()
    for step in range(rows):
        f = first_at(step)
        load(f, 0).start()
        load(f, 1).start()
    for step in range(rows):
        load(send_at(step), 2).start()

    barrier = pltpu.get_barrier_semaphore()

    def greet_at(i, j):
        pl.semaphore_signal(barrier, inc=1, device_id=(i, j), device_id_type=MESH)

    def tell(sem, j):
        pl.semaphore_signal(sem, inc=1, device_id=(ia, j), device_id_type=MESH)

    @pl.when(core == 0)
    def _():
        greet_at(ia, ja + 1)

        @pl.when(ja > 0)
        def _():
            greet_at(ia, ja - 1)

    def greet_chips(step, carry):
        peer = (me // 2 + step) % (total // 2) * 2
        greet_at(peer // n_ja, peer % n_ja)
        return carry

    lax.fori_loop(1, total // 2, greet_chips, 0)

    @pl.when(ja == 0)
    def _():
        left[...] = jnp.zeros_like(left)

    @pl.when(ja == n_ja - 1)
    def _():
        right[...] = jnp.zeros_like(right)

    def to_right(sweep, f):
        return pltpu.make_async_remote_copy(
            src_ref=xl.at[f, pl.ds(cols - WIN, WIN)],
            dst_ref=left.at[sweep, f],
            send_sem=halo_send.at[0, f],
            recv_sem=halo_recv.at[sweep, 0, f],
            device_id=(ia, jnp.minimum(ja + 1, n_ja - 1)),
            device_id_type=MESH,
        )

    def to_left(sweep, f):
        return pltpu.make_async_remote_copy(
            src_ref=xl.at[f, pl.ds(0, WIN)],
            dst_ref=right.at[sweep, f],
            send_sem=halo_send.at[1, f],
            recv_sem=halo_recv.at[sweep, 1, f],
            device_id=(ia, jnp.maximum(ja - 1, 0)),
            device_id_type=MESH,
        )

    def start_halo(sweep, f):
        @pl.when(ja < n_ja - 1)
        def _():
            to_right(sweep, f).start()

        @pl.when(ja > 0)
        def _():
            to_left(sweep, f).start()

    def wait_halo(sweep, f):
        @pl.when(ja > 0)
        def _():
            to_right(sweep, f).wait_recv()

        @pl.when(ja < n_ja - 1)
        def _():
            to_left(sweep, f).wait_recv()

    def wait_halo_sends(sweep, f):
        @pl.when(ja < n_ja - 1)
        def _():
            to_right(sweep, f).wait_send()

        @pl.when(ja > 0)
        def _():
            to_left(sweep, f).wait_send()

    def pair_copy(sweep, f, c):
        return pltpu.make_async_remote_copy(
            src_ref=hs.at[f, c],
            dst_ref=hr.at[sweep, ja, ia],
            send_sem=pair_send.at[f, c],
            recv_sem=pair_recv.at[sweep, ja],
            device_id=(c, f),
            device_id_type=MESH,
        )

    def start_pair(sweep, f, c):
        own = (f == ja) & (c == ia)

        @pl.when(jnp.logical_not(own))
        def _():
            pair_copy(sweep, f, c).start()

        @pl.when(own)
        def _():
            pltpu.make_async_copy(
                hs.at[f, c], hr.at[sweep, ja, ia], pair_recv.at[sweep, ja]
            ).start()

    def wait_pair_row(sweep, f):
        pltpu.make_async_copy(hr.at[sweep, f], hr.at[sweep, f], pair_recv.at[sweep, f]).wait()

    def wait_pair_sends(sweep, f):
        for c in range(cols):
            @pl.when(jnp.logical_not((f == ja) & (c == ia)))
            def _():
                pair_copy(sweep, f, c).wait_send()

    def back_form(f, group):
        lead = [dot(c_ref[f, c], out_ref[f, c]).astype(BF16) for c in group]
        for y, c in zip(lead, group):
            xl[f, c] = dot(y, ct[f, c]).astype(BF16)

    def inside(f, c):
        count = cnt_ref[f, c]
        p = lax.broadcasted_iota(jnp.int32, (size, size), 0)
        q = lax.broadcasted_iota(jnp.int32, (size, size), 1)
        return (p < count) & (q < count)

    def meet_neighbours():
        @pl.when(core == 1)
        def _():
            pl.semaphore_wait(barrier, jnp.where(ja + 1 < n_ja, 2, 1))
            tell(near_sem, ja - 1)

            @pl.when(ja + 1 < n_ja)
            def _():
                tell(near_sem, ja + 1)

        @pl.when(core == 0)
        def _():
            pl.semaphore_wait(near_sem, jnp.where(ja > 0, 2, 1))

    def meet_all():
        @pl.when(core == 0)
        def _():
            pl.semaphore_wait(barrier, total - 2)
            tell(go_sem, ja + 1)

        @pl.when(core == 1)
        def _():
            pl.semaphore_wait(go_sem, 1)

    def first_rows(step, carry):
        f = first_at(step)
        load(f, 0).wait()
        load(f, 1).wait()
        for group in groups:
            for c in group:
                t = out_ref[f, c]
                out_ref[f, c] = jnp.where(inside(f, c), t, jnp.zeros_like(t))
                ct[f, c] = c_ref[f, c].T
            back_form(f, group)

        @pl.when(step == 0)
        def _():
            meet_neighbours()

        start_halo(0, f)
        return carry

    for copy in small:
        copy.wait()
    lax.fori_loop(0, rows, first_rows, 0)

    def gain_row(step, carry):
        f = step
        columns_e = e_ref[f].T
        for c in range(cols):
            shift = occ_ref[f * n_ia + ia] + occ_ref[ja * cols + c]
            denominator = columns_e[:, c : c + 1] + e_ref[f, pl.ds(c, 1)] - shift
            gain[f, c] = jnp.where(inside(f, c), DAMPING / denominator, 0.0)
        return carry

    def quad_row(f):
        for group in groups:
            z = [dot(out_ref[f, c], k_ref[f, c]).astype(BF16) for c in group]
            for left_quad, c in zip(z, group):
                hq[f, c] = 0.5 * k_ref[f, c].astype(F32) + dot(left_quad, out_ref[f, c]) * (1.0 / size)

    def half_row(sweep, at, send, step, carry):
        f = at(step)
        wait_halo(sweep, f)
        if sweep > 0:
            wait_pair_sends(sweep - 1, f)
        def run(group):
            sums = []
            for c in group:
                acc = None
                j = ja * cols + c
                for slot in range(2 * WIN):
                    d = window_shift(slot)
                    k = j + d
                    ok = (k >= 0) & (k < orbitals)
                    kc = jnp.clip(k, 0, orbitals - 1)
                    w = cpl_ref[f, c, slot].astype(F32) * fock_ref[kc, j]
                    w = jnp.where(ok, w, 0.0)
                    at = c + d
                    if at < 0:
                        x = left[sweep, f, at + WIN]
                    elif at >= cols:
                        x = right[sweep, f, at - cols]
                    else:
                        x = xl[f, at]
                    term = w * x.astype(F32)
                    acc = term if acc is None else acc + term
                sums.append(acc.astype(BF16))
            proj = [dot(ct[f, c], a).astype(BF16) for a, c in zip(sums, group)]
            for b, c in zip(proj, group):
                hs[f, c] = (hq[f, c] - dot(b, c_ref[f, c])).astype(BF16)
            @pl.when(send)
            def _():
                for c in group:
                    start_pair(sweep, f, c)

        for group in groups:
            run(group)
        return carry

    def update_row(sweep, at, step, carry):
        f = at(step)
        wait_pair_row(sweep, f)
        if sweep < ITERS - 1:
            wait_halo_sends(sweep, f)
        for group in groups:
            for c in group:
                resid = hs[f, c].astype(F32) + hr[sweep, f, c].T.astype(F32)
                out_ref[f, c] = (
                    (1.0 - DAMPING) * out_ref[f, c].astype(F32) - gain[f, c] * resid
                ).astype(BF16)
            if sweep < ITERS - 1:
                back_form(f, group)
        if sweep < ITERS - 1:
            start_halo(sweep + 1, f)
        return carry

    def first_half(sent, step, carry):
        f = send_at(step)
        load(f, 2).wait()
        quad_row(f)
        return half_row(0, send_at, step < sent, step, carry)

    def send_row(sweep, f):
        for c in mixed:
            start_pair(sweep, f, c)

    def quad_at(at, step, carry):
        quad_row(at(step))
        return carry

    def each(body, *args):
        lax.fori_loop(0, half_ja, functools.partial(body, *args), 0)

    meet_all()
    sent = jnp.where(border, rows, rows - 1)
    lax.fori_loop(0, rows, functools.partial(first_half, sent), 0)
    lax.fori_loop(0, rows, gain_row, 0)

    def send_held(step, carry):
        send_row(0, send_at(step))
        return carry

    for sweep in range(ITERS - 1):
        each(update_row, sweep, own_at)
        if sweep == 0:
            lax.fori_loop(sent, rows, send_held, 0)

        @pl.when(border)
        def _():
            each(update_row, sweep, across_at)

        each(quad_at, own_at)
        each(half_row, sweep + 1, own_at, True)

        @pl.when(jnp.logical_not(border))
        def _():
            each(update_row, sweep, across_at)

        each(quad_at, across_at)
        each(half_row, sweep + 1, across_end_at, True)
    lax.fori_loop(0, rows, functools.partial(update_row, ITERS - 1, last_at), 0)

    def finish(f, carry):
        wait_halo_sends(ITERS - 1, f)
        wait_pair_sends(ITERS - 1, f)
        return carry

    lax.fori_loop(0, rows, finish, 0)


def solution(mesh):
    n_ia, n_ja = mesh.shape["ia"], mesh.shape["ja"]

    def on_device(amps, coefs, ints, energy, counts, coupled, occ_fock, occ_energy):
        rows, _, cols, size, _ = amps.shape
        assert rows == n_ja and cols == n_ia and cols >= WIN and n_ja % 2 == 0
        pairs = (rows, cols, size, size)
        unit = 2 * rows * cols * size * size
        halo = 2 * ITERS * unit * WIN // cols
        limit = min(67043328, (9 + ITERS) * unit + halo + (4 << 20))
        out = pl.pallas_call(
            functools.partial(sweeps_kernel, n_ia, n_ja),
            out_shape=pltpu.VMEM(pairs, BF16),
            in_specs=[pl.BlockSpec(memory_space=pltpu.HBM)] * 8,
            out_specs=pl.BlockSpec(memory_space=pltpu.VMEM),
            scratch_shapes=[
                pltpu.VMEM(pairs, BF16),
                pltpu.VMEM(pairs, BF16),
                pltpu.VMEM((rows, cols, size), F32),
                pltpu.SMEM((rows, cols), jnp.int32),
                pltpu.SMEM((rows, cols, 2 * WIN), jnp.int32),
                pltpu.SMEM(occ_fock.shape, F32),
                pltpu.SMEM(occ_energy.shape, F32),
                pltpu.VMEM(pairs, BF16),
                pltpu.VMEM(pairs, BF16),
                pltpu.VMEM((ITERS, rows, WIN, size, size), BF16),
                pltpu.VMEM((ITERS, rows, WIN, size, size), BF16),
                pltpu.VMEM(pairs, F32),
                pltpu.VMEM(pairs, F32),
                pltpu.VMEM(pairs, BF16),
                pltpu.VMEM((ITERS,) + pairs, BF16),
                pltpu.SemaphoreType.DMA((2, rows)),
                pltpu.SemaphoreType.DMA((ITERS, 2, rows)),
                pltpu.SemaphoreType.DMA((rows, cols)),
                pltpu.SemaphoreType.DMA((ITERS, rows)),
                pltpu.SemaphoreType.DMA((3, rows)),
                pltpu.SemaphoreType.DMA((5,)),
                pltpu.SemaphoreType.REGULAR,
                pltpu.SemaphoreType.REGULAR,
            ],
            compiler_params=pltpu.CompilerParams(
                collective_id=0, has_side_effects=True, vmem_limit_bytes=limit
            ),
        )(*[
            pltpu.with_memory_space_constraint(x, pltpu.HBM)
            for x in (
                amps.reshape(pairs),
                coefs.reshape(pairs),
                ints.reshape(pairs),
                energy.reshape(rows, cols, size),
                counts.reshape(rows, cols),
                coupled.reshape(rows, cols, 2 * WIN),
                occ_fock,
                occ_energy,
            )
        ])
        return out.reshape(amps.shape)

    placed = (
        P(None, "ia", "ja", None, None),
        P(None, "ia", "ja", None, None),
        P(None, "ia", "ja", None, None),
        P(None, "ia", "ja", None),
        P(None, "ia", "ja"),
        P(None, "ia", "ja", None),
        P(),
        P(),
    )
    return jax.shard_map(
        on_device,
        mesh=mesh,
        in_specs=placed,
        out_specs=P(None, "ia", "ja", None, None),
        check_vma=False,
    )
```

```python
import functools

import jax
import jax.numpy as jnp
from jax import lax
from jax.experimental import pallas as pl
from jax.experimental.pallas import tpu as pltpu
from jax.sharding import PartitionSpec as P

WIN = 6
ITERS = 2
DAMPING = 0.5
GROUP = 4
MESH = pl.DeviceIdType.MESH
F32 = jnp.float32
BF16 = jnp.bfloat16


def window_shift(slot):
    return slot - WIN if slot < WIN else slot - WIN + 1


def dot(a, b):
    return jnp.dot(a, b, preferred_element_type=F32)


def sweeps_kernel(
    n_ia, n_ja,
    t_hbm, c_hbm, k_hbm, e_hbm, cnt_hbm, cpl_hbm, fock_hbm, occ_hbm,
    out_ref,
    c_ref, k_ref, e_ref, cnt_ref, cpl_ref, fock_ref, occ_ref,
    ct, xl, left, right, hq, gain, hs, hr,
    halo_send, halo_recv, pair_send, pair_recv, load_sem, small_sem, near_sem, go_sem,
):
    rows, cols, size, _ = out_ref.shape
    orbitals = occ_ref.shape[0]
    ia = lax.axis_index("ia")
    ja = lax.axis_index("ja")
    me = ia * n_ja + ja
    total = n_ia * n_ja
    mixed = [n // 2 + n % 2 * (cols // 2) for n in range(cols)]
    groups = [mixed[g : g + GROUP] for g in range(0, cols, GROUP)]
    core = ja % 2
    half_ja = n_ja // 2
    low = ja < half_ja
    border = (ja == half_ja - 1) | (ja == half_ja)

    def flipped(turn, f):
        return jnp.where(turn, n_ja - 1 - f, f)

    def middle_out(step):
        return half_ja + jnp.where(step % 2 == 0, -1 - step // 2, step // 2)

    def first_at(step):
        return flipped(low == border, middle_out(step))

    def send_at(step):
        return flipped(jnp.logical_not(low), middle_out(step))

    def own_at(step):
        return flipped(jnp.logical_not(low), step)

    def across_at(step):
        return flipped(jnp.logical_not(low), half_ja + step)

    def across_end_at(step):
        return across_at(jnp.where(border, half_ja - 1 - step, step))

    def last_at(step):
        return flipped(jnp.logical_not(low), jnp.where(step < half_ja, step, n_ja - 1 - step + half_ja))

    small = [
        pltpu.make_async_copy(src, dst, small_sem.at[n])
        for n, (src, dst) in enumerate(
            [(cnt_hbm, cnt_ref), (cpl_hbm, cpl_ref), (fock_hbm, fock_ref),
             (occ_hbm, occ_ref), (e_hbm, e_ref)]
        )
    ]

    def load(f, n):
        src, dst = [(t_hbm, out_ref), (c_hbm, c_ref), (k_hbm, k_ref)][n]
        return pltpu.make_async_copy(src.at[f], dst.at[f], load_sem.at[n, f])

    for copy in small:
        copy.start()
    for step in range(rows):
        f = first_at(step)
        load(f, 0).start()
        load(f, 1).start()
    for step in range(rows):
        load(send_at(step), 2).start()

    barrier = pltpu.get_barrier_semaphore()

    def greet_at(i, j):
        pl.semaphore_signal(barrier, inc=1, device_id=(i, j), device_id_type=MESH)

    def tell(sem, j):
        pl.semaphore_signal(sem, inc=1, device_id=(ia, j), device_id_type=MESH)

    @pl.when(core == 0)
    def _():
        greet_at(ia, ja + 1)

        @pl.when(ja > 0)
        def _():
            greet_at(ia, ja - 1)

    def greet_chips(step, carry):
        peer = (me // 2 + step) % (total // 2) * 2
        greet_at(peer // n_ja, peer % n_ja)
        return carry

    lax.fori_loop(1, total // 2, greet_chips, 0)

    @pl.when(ja == 0)
    def _():
        left[...] = jnp.zeros_like(left)

    @pl.when(ja == n_ja - 1)
    def _():
        right[...] = jnp.zeros_like(right)

    def to_right(sweep, f):
        return pltpu.make_async_remote_copy(
            src_ref=xl.at[f, pl.ds(cols - WIN, WIN)],
            dst_ref=left.at[sweep, f],
            send_sem=halo_send.at[0, f],
            recv_sem=halo_recv.at[sweep, 0, f],
            device_id=(ia, jnp.minimum(ja + 1, n_ja - 1)),
            device_id_type=MESH,
        )

    def to_left(sweep, f):
        return pltpu.make_async_remote_copy(
            src_ref=xl.at[f, pl.ds(0, WIN)],
            dst_ref=right.at[sweep, f],
            send_sem=halo_send.at[1, f],
            recv_sem=halo_recv.at[sweep, 1, f],
            device_id=(ia, jnp.maximum(ja - 1, 0)),
            device_id_type=MESH,
        )

    def start_halo(sweep, f):
        @pl.when(ja < n_ja - 1)
        def _():
            to_right(sweep, f).start()

        @pl.when(ja > 0)
        def _():
            to_left(sweep, f).start()

    def wait_halo(sweep, f):
        @pl.when(ja > 0)
        def _():
            to_right(sweep, f).wait_recv()

        @pl.when(ja < n_ja - 1)
        def _():
            to_left(sweep, f).wait_recv()

    def wait_halo_sends(sweep, f):
        @pl.when(ja < n_ja - 1)
        def _():
            to_right(sweep, f).wait_send()

        @pl.when(ja > 0)
        def _():
            to_left(sweep, f).wait_send()

    def pair_copy(sweep, f, c):
        return pltpu.make_async_remote_copy(
            src_ref=hs.at[f, c],
            dst_ref=hr.at[sweep, ja, ia],
            send_sem=pair_send.at[f, c],
            recv_sem=pair_recv.at[sweep, ja],
            device_id=(c, f),
            device_id_type=MESH,
        )

    def start_pair(sweep, f, c):
        own = (f == ja) & (c == ia)

        @pl.when(jnp.logical_not(own))
        def _():
            pair_copy(sweep, f, c).start()

        @pl.when(own)
        def _():
            pltpu.make_async_copy(
                hs.at[f, c], hr.at[sweep, ja, ia], pair_recv.at[sweep, ja]
            ).start()

    def wait_pair_row(sweep, f):
        pltpu.make_async_copy(hr.at[sweep, f], hr.at[sweep, f], pair_recv.at[sweep, f]).wait()

    def wait_pair_sends(sweep, f):
        for c in range(cols):
            @pl.when(jnp.logical_not((f == ja) & (c == ia)))
            def _():
                pair_copy(sweep, f, c).wait_send()

    def back_form(f, group):
        lead = [dot(c_ref[f, c], out_ref[f, c]).astype(BF16) for c in group]
        for y, c in zip(lead, group):
            xl[f, c] = dot(y, ct[f, c]).astype(BF16)

    def inside(f, c):
        count = cnt_ref[f, c]
        p = lax.broadcasted_iota(jnp.int32, (size, size), 0)
        q = lax.broadcasted_iota(jnp.int32, (size, size), 1)
        return (p < count) & (q < count)

    def meet_neighbours():
        @pl.when(core == 1)
        def _():
            pl.semaphore_wait(barrier, jnp.where(ja + 1 < n_ja, 2, 1))
            tell(near_sem, ja - 1)

            @pl.when(ja + 1 < n_ja)
            def _():
                tell(near_sem, ja + 1)

        @pl.when(core == 0)
        def _():
            pl.semaphore_wait(near_sem, jnp.where(ja > 0, 2, 1))

    def pass_on():
        @pl.when(core == 0)
        def _():
            pl.semaphore_wait(barrier, total - 2)
            tell(go_sem, ja + 1)

    def meet_all():
        @pl.when(core == 1)
        def _():
            pl.semaphore_wait(go_sem, 1)

    def first_rows(step, carry):
        f = first_at(step)
        load(f, 0).wait()
        load(f, 1).wait()
        for group in groups:
            for c in group:
                t = out_ref[f, c]
                out_ref[f, c] = jnp.where(inside(f, c), t, jnp.zeros_like(t))
                ct[f, c] = c_ref[f, c].T
            back_form(f, group)

        @pl.when(step == rows - 1)
        def _():
            pass_on()

        @pl.when(step == 0)
        def _():
            meet_neighbours()

        start_halo(0, f)
        return carry

    for copy in small:
        copy.wait()
    lax.fori_loop(0, rows, first_rows, 0)

    def gain_row(step, carry):
        f = step
        columns_e = e_ref[f].T
        for c in range(cols):
            shift = occ_ref[f * n_ia + ia] + occ_ref[ja * cols + c]
            denominator = columns_e[:, c : c + 1] + e_ref[f, pl.ds(c, 1)] - shift
            gain[f, c] = jnp.where(inside(f, c), DAMPING / denominator, 0.0)
        return carry

    def quad_row(f):
        for group in groups:
            z = [dot(out_ref[f, c], k_ref[f, c]).astype(BF16) for c in group]
            for left_quad, c in zip(z, group):
                hq[f, c] = 0.5 * k_ref[f, c].astype(F32) + dot(left_quad, out_ref[f, c]) * (1.0 / size)

    def half_row(sweep, at, send, step, carry):
        f = at(step)
        wait_halo(sweep, f)
        if sweep > 0:
            wait_pair_sends(sweep - 1, f)
        def run(group):
            sums = []
            for c in group:
                acc = None
                j = ja * cols + c
                for slot in range(2 * WIN):
                    d = window_shift(slot)
                    k = j + d
                    ok = (k >= 0) & (k < orbitals)
                    kc = jnp.clip(k, 0, orbitals - 1)
                    w = cpl_ref[f, c, slot].astype(F32) * fock_ref[kc, j]
                    w = jnp.where(ok, w, 0.0)
                    at = c + d
                    if at < 0:
                        x = left[sweep, f, at + WIN]
                    elif at >= cols:
                        x = right[sweep, f, at - cols]
                    else:
                        x = xl[f, at]
                    term = w * x.astype(F32)
                    acc = term if acc is None else acc + term
                sums.append(acc.astype(BF16))
            proj = [dot(ct[f, c], a).astype(BF16) for a, c in zip(sums, group)]
            for b, c in zip(proj, group):
                hs[f, c] = (hq[f, c] - dot(b, c_ref[f, c])).astype(BF16)
            @pl.when(send)
            def _():
                for c in group:
                    start_pair(sweep, f, c)

        for group in groups:
            run(group)
        return carry

    def update_row(sweep, at, step, carry):
        f = at(step)
        wait_pair_row(sweep, f)
        if sweep < ITERS - 1:
            wait_halo_sends(sweep, f)
        for group in groups:
            for c in group:
                resid = hs[f, c].astype(F32) + hr[sweep, f, c].T.astype(F32)
                out_ref[f, c] = (
                    (1.0 - DAMPING) * out_ref[f, c].astype(F32) - gain[f, c] * resid
                ).astype(BF16)
            if sweep < ITERS - 1:
                back_form(f, group)
        if sweep < ITERS - 1:
            start_halo(sweep + 1, f)
        return carry

    def first_half(sent, step, carry):
        f = send_at(step)
        load(f, 2).wait()
        quad_row(f)
        return half_row(0, send_at, step < sent, step, carry)

    def send_row(sweep, f):
        for c in mixed:
            start_pair(sweep, f, c)

    def quad_at(at, step, carry):
        quad_row(at(step))
        return carry

    def each(body, *args):
        lax.fori_loop(0, half_ja, functools.partial(body, *args), 0)

    meet_all()
    sent = jnp.where(border, rows, rows - 1)
    lax.fori_loop(0, rows, functools.partial(first_half, sent), 0)
    lax.fori_loop(0, rows, gain_row, 0)

    def send_held(step, carry):
        send_row(0, send_at(step))
        return carry

    for sweep in range(ITERS - 1):
        each(update_row, sweep, own_at)
        if sweep == 0:
            lax.fori_loop(sent, rows, send_held, 0)

        @pl.when(border)
        def _():
            each(update_row, sweep, across_at)

        each(quad_at, own_at)
        each(half_row, sweep + 1, own_at, True)

        @pl.when(jnp.logical_not(border))
        def _():
            each(update_row, sweep, across_at)

        each(quad_at, across_at)
        each(half_row, sweep + 1, across_end_at, True)
    lax.fori_loop(0, rows, functools.partial(update_row, ITERS - 1, last_at), 0)

    def finish(f, carry):
        wait_halo_sends(ITERS - 1, f)
        wait_pair_sends(ITERS - 1, f)
        return carry

    lax.fori_loop(0, rows, finish, 0)


def solution(mesh):
    n_ia, n_ja = mesh.shape["ia"], mesh.shape["ja"]

    def on_device(amps, coefs, ints, energy, counts, coupled, occ_fock, occ_energy):
        rows, _, cols, size, _ = amps.shape
        assert rows == n_ja and cols == n_ia and cols >= WIN and n_ja % 2 == 0
        pairs = (rows, cols, size, size)
        unit = 2 * rows * cols * size * size
        halo = 2 * ITERS * unit * WIN // cols
        limit = min(67043328, (9 + ITERS) * unit + halo + (4 << 20))
        out = pl.pallas_call(
            functools.partial(sweeps_kernel, n_ia, n_ja),
            out_shape=pltpu.VMEM(pairs, BF16),
            in_specs=[pl.BlockSpec(memory_space=pltpu.HBM)] * 8,
            out_specs=pl.BlockSpec(memory_space=pltpu.VMEM),
            scratch_shapes=[
                pltpu.VMEM(pairs, BF16),
                pltpu.VMEM(pairs, BF16),
                pltpu.VMEM((rows, cols, size), F32),
                pltpu.SMEM((rows, cols), jnp.int32),
                pltpu.SMEM((rows, cols, 2 * WIN), jnp.int32),
                pltpu.SMEM(occ_fock.shape, F32),
                pltpu.SMEM(occ_energy.shape, F32),
                pltpu.VMEM(pairs, BF16),
                pltpu.VMEM(pairs, BF16),
                pltpu.VMEM((ITERS, rows, WIN, size, size), BF16),
                pltpu.VMEM((ITERS, rows, WIN, size, size), BF16),
                pltpu.VMEM(pairs, F32),
                pltpu.VMEM(pairs, F32),
                pltpu.VMEM(pairs, BF16),
                pltpu.VMEM((ITERS,) + pairs, BF16),
                pltpu.SemaphoreType.DMA((2, rows)),
                pltpu.SemaphoreType.DMA((ITERS, 2, rows)),
                pltpu.SemaphoreType.DMA((rows, cols)),
                pltpu.SemaphoreType.DMA((ITERS, rows)),
                pltpu.SemaphoreType.DMA((3, rows)),
                pltpu.SemaphoreType.DMA((5,)),
                pltpu.SemaphoreType.REGULAR,
                pltpu.SemaphoreType.REGULAR,
            ],
            compiler_params=pltpu.CompilerParams(
                collective_id=0, has_side_effects=True, vmem_limit_bytes=limit
            ),
        )(*[
            pltpu.with_memory_space_constraint(x, pltpu.HBM)
            for x in (
                amps.reshape(pairs),
                coefs.reshape(pairs),
                ints.reshape(pairs),
                energy.reshape(rows, cols, size),
                counts.reshape(rows, cols),
                coupled.reshape(rows, cols, 2 * WIN),
                occ_fock,
                occ_energy,
            )
        ])
        return out.reshape(amps.shape)

    placed = (
        P(None, "ia", "ja", None, None),
        P(None, "ia", "ja", None, None),
        P(None, "ia", "ja", None, None),
        P(None, "ia", "ja", None),
        P(None, "ia", "ja"),
        P(None, "ia", "ja", None),
        P(),
        P(),
    )
    return jax.shard_map(
        on_device,
        mesh=mesh,
        in_specs=placed,
        out_specs=P(None, "ia", "ja", None, None),
        check_vma=False,
    )
```
